32 devices in a mesh: ctx: 16 (over z, x, core), chan: 2 (over y).
Axes of the slice: x: 2, y: 2, z: 4, core: 2. Of those that a mesh axis runs over, the one named last changes fastest.
Arguments:
- gated_input: bfloat16 [4096, 8192], P('ctx', 'chan'), may hold values from -6 to 6
- query: bfloat16 [4096, 8192], P('ctx', 'chan'), may hold values from -6 to 6
- out_grad: bfloat16 [4096, 8192], P('ctx', 'chan'), may hold values from -6 to 6
- out_weight: bfloat16 [8192, 8192], P('chan', 'ctx'), may hold values from -0.0625 to 0.0625
- decay_rate: float32 [16, 8192], P(None, 'chan'), may hold values from 2.4414063e-05 to 0.083333333
- residue: float32 [16, 8192], P(None, 'chan'), may hold values from -0.5 to 0.5
Outputs:
- grad_query: bfloat16 [4096, 8192], P('ctx', 'chan')
- grad_input: bfloat16 [4096, 8192], P('ctx', 'chan')
The draws below stay inside these ranges and needn't reach their ends.
All inputs are finite; a program needn't handle non-finite values.
Results may differ from the reference program's by a relative error of at most 0.0013.
Values may be sent and summed in bfloat16 or wider, within the bound.
A program may use at most 576 MiB of HBM per device.

```python
import math
import jax
import jax.numpy as jnp

D = 8192
MODES = 16
SEQ = 4096


def draw_filter(key):
    base_key = jax.random.fold_in(key, 7)
    kind_key, slow_key, middle_key, fast_key, sign_key = jax.random.split(base_key, 5)
    grid_shape = (MODES, D)
    mode_kinds = jax.random.randint(kind_key, grid_shape, 0, 8)

    def spread(sub_key, lower, upper):
        return jnp.exp(jax.random.uniform(sub_key, grid_shape, jnp.float32, math.log(lower), math.log(upper)))
    slow_rate = spread(slow_key, 0.1 / SEQ, 1.5 / SEQ)
    middle_rate = spread(middle_key, 1.5 / SEQ, 1.0 / 64)
    fast_rate = spread(fast_key, 1.0 / 40, 1.0 / 12)
    decay = jnp.where(mode_kinds < 4, slow_rate, jnp.where(mode_kinds < 6, middle_rate, fast_rate))
    amplitude = jax.random.truncated_normal(sign_key, -4.0, 4.0, grid_shape, jnp.float32)
    weights = amplitude * jnp.sqrt(2.0 * decay / MODES)
    return (decay, weights)


def draw_decay_rate(key, part):
    return draw_filter(key)[0]


def draw_residue(key, part):
    return draw_filter(key)[1]


def block_scale(rng, dims, shards, low, largest):
    factor_of, own = 1.0, jax.random.fold_in(rng, 6)
    for position, blocks in shards:
        steps = jnp.exp(jax.random.uniform(jax.random.fold_in(own, position), (blocks,), jnp.float32, low / len(shards), largest / len(shards)))
        factor_of = factor_of * jnp.repeat(steps, dims[position] // blocks).reshape([-1 if axis == position else 1 for axis in range(len(dims))])
    return factor_of


def normal_values(stream_key, dims, scale, reach, cuts=(), kind=jnp.bfloat16):
    values = jax.random.normal(stream_key, dims, jnp.float32) * scale
    if len(cuts) > 0:
        values = block_scale(stream_key, dims, cuts, -0.22, 0.18) * values
    return jnp.clip(values, min=-reach, max=reach).astype(kind)


def setup_inputs(seed: int = 0) -> dict:
    key_of = jax.random.split(jax.random.key(seed), 7)
    gated_input = normal_values(key_of[0], (SEQ, D), 1.0, 6.0, ((0, 16), (1, 2)))
    query = normal_values(key_of[1], (SEQ, D), 1.0, 6.0, ((0, 16), (1, 2)))
    out_grad = normal_values(key_of[2], (SEQ, D), 1.0, 6.0, ((0, 16), (1, 2)))
    out_weight = normal_values(key_of[3], (D, D), D ** -0.5, 0.0625, ((0, 2), (1, 16)))
    decay_rate = draw_decay_rate(jax.random.fold_in(key_of[6], 71), 0)
    residue = draw_residue(jax.random.fold_in(key_of[6], 71), 0)
    return {"gated_input": gated_input, "query": query, "out_grad": out_grad, "out_weight": out_weight, "decay_rate": decay_rate, "residue": residue}


def causal_conv(signal, kernel):
    length = signal.shape[0]
    total = signal.shape[1]
    span = min(total, 1024)
    pieces = []
    for first in range(0, total, span):
        sig_block = signal[:, first:first + span]
        ker_block = kernel[:, first:first + span]
        spectrum = jnp.fft.rfft(sig_block, 2 * length, axis=0) * jnp.fft.rfft(ker_block, 2 * length, axis=0)
        pieces.append(jnp.fft.irfft(spectrum, 2 * length, axis=0)[:length])
    return jnp.concatenate(pieces, axis=1)


def reference(gated_input, query, out_grad, out_weight, decay_rate, residue):
    lag_steps = jnp.arange(SEQ, dtype=jnp.float32)[:, None]
    filter_taps = jnp.zeros((SEQ, D), jnp.float32)
    for mode_index in range(MODES):
        filter_taps = filter_taps + residue[mode_index][None, :] * jnp.exp(-decay_rate[mode_index][None, :] * lag_steps)
    conv_out = causal_conv(gated_input.astype(jnp.float32), filter_taps)
    grad_mixed = jnp.dot(out_grad, out_weight.T, preferred_element_type=jnp.float32)
    grad_query = (grad_mixed * conv_out).astype(jnp.bfloat16)
    grad_conv = grad_mixed * query.astype(jnp.float32)
    grad_input = causal_conv(grad_conv[::-1], filter_taps)[::-1]
    return grad_query, grad_input.astype(jnp.bfloat16)
```

```python
import jax
import jax.numpy as jnp
import numpy as np
from jax import lax
from jax.sharding import PartitionSpec as P

block_rows = 64
full_precision = lax.Precision.HIGHEST


def passed_along(value, axis, steps):
    count = lax.axis_size(axis)
    initial, last = (max(0, -steps), min(count, count - steps))
    return lax.ppermute(value, axis, [(source, source + steps) for source in range(initial, last)])


def prefix_scan(value, decay_one, axis, direction):
    count = lax.axis_size(axis)
    state = passed_along(value, axis, direction)
    factor, step = decay_one, 1
    while step < count:
        state = state + factor * passed_along(state, axis, step * direction)
        factor, step = factor * factor, step * 2
    return state


def on_device(gated_input, query, out_grad, out_weight, decay_rate, residue):
    tok_rows, chan_width = gated_input.shape
    block_count = tok_rows // block_rows
    lag_steps = jnp.arange(block_rows, dtype=jnp.float32)
    filter_taps = jnp.sum(
        residue[None] * jnp.exp(-decay_rate[None] * lag_steps[:, None, None]), axis=1
    )
    lag_offsets = np.arange(block_rows)[:, None] - np.arange(block_rows)[None, :]
    lag_table = np.where(lag_offsets >= 0, lag_offsets, block_rows).reshape(-1).astype(np.int32)
    padded_taps = jnp.concatenate([filter_taps, jnp.zeros((1, chan_width), jnp.float32)], axis=0)
    toeplitz = jnp.take(padded_taps, jnp.asarray(lag_table), axis=0).reshape(
        block_rows, block_rows, chan_width
    )
    to_end = jnp.exp(-decay_rate[None] * (block_rows - 1.0 - lag_steps)[:, None, None])
    from_start = jnp.exp(-decay_rate[None] * lag_steps[:, None, None])
    into_rows = residue[None] * jnp.exp(-decay_rate[None] * (lag_steps + 1.0)[:, None, None])
    back_rows = residue[None] * jnp.exp(-decay_rate[None] * (block_rows - lag_steps)[:, None, None])
    block_index = jnp.arange(block_count, dtype=jnp.float32)
    state_index = jnp.arange(block_count + 1, dtype=jnp.float32)
    gap_blocks = state_index[:, None] - 1.0 - block_index[None, :]
    fwd_coef = jnp.where(
        (gap_blocks >= 0.0)[:, :, None, None],
        jnp.exp(
            -decay_rate[None, None] * block_rows * jnp.maximum(gap_blocks, 0.0)[:, :, None, None]
        ),
        0.0,
    )
    back_coef = fwd_coef[::-1, ::-1]
    chain_decay = jnp.exp(-decay_rate * tok_rows)
    zero_state = jnp.zeros_like(chain_decay)
    input_blocks = gated_input.astype(jnp.float32).reshape(block_count, block_rows, chan_width)
    local_part = jnp.einsum("tsc,nsc->ntc", toeplitz, input_blocks, precision=full_precision)
    block_ends = jnp.einsum("smc,nsc->nmc", to_end, input_blocks, precision=full_precision)
    block_states = jnp.einsum("nkmc,kmc->nmc", fwd_coef, block_ends, precision=full_precision)
    local_end = block_states[block_count]

    earlier_state = prefix_scan(local_end, chain_decay, "ctx", 1)
    start_states = (
        block_states[:block_count]
        + jnp.exp(-decay_rate[None] * block_rows * block_index[:, None, None]) * earlier_state[None]
    )
    carried = jnp.einsum("tmc,nmc->ntc", into_rows, start_states, precision=full_precision)
    conv_out = (local_part + carried).reshape(tok_rows, chan_width)
    grad_rows = lax.all_gather(out_grad, "chan", axis=1, tiled=True)
    grad_mixed = lax.dot_general(
        grad_rows,
        lax.all_gather(out_weight, "ctx", axis=1, tiled=True),
        (((1,), (1,)), ((), ())),
        preferred_element_type=jnp.float32,
    )
    grad_query = (grad_mixed * conv_out).astype(jnp.bfloat16)
    grad_conv = (grad_mixed * query.astype(jnp.float32)).reshape(
        block_count, block_rows, chan_width
    )
    local_back = jnp.einsum("tsc,ntc->nsc", toeplitz, grad_conv, precision=full_precision)
    block_heads = jnp.einsum("tmc,ntc->nmc", from_start, grad_conv, precision=full_precision)
    block_tails = jnp.einsum("nkmc,kmc->nmc", back_coef, block_heads, precision=full_precision)
    local_out = block_tails[0]

    later_state = prefix_scan(local_out, chain_decay, "ctx", -1)
    end_states = (
        block_tails[1:]
        + jnp.exp(-decay_rate[None] * block_rows * (block_count - 1.0 - block_index)[:, None, None])
        * later_state[None]
    )
    carried_back = jnp.einsum("smc,nmc->nsc", back_rows, end_states, precision=full_precision)
    grad_input = (local_back + carried_back).reshape(tok_rows, chan_width).astype(jnp.bfloat16)
    return (grad_query, grad_input)


def solution(mesh):
    return jax.shard_map(
        on_device,
        mesh=mesh,
        in_specs=(
            P("ctx", "chan"),
            P("ctx", "chan"),
            P("ctx", "chan"),
            P("chan", "ctx"),
            P(None, "chan"),
            P(None, "chan"),
        ),
        out_specs=(P("ctx", "chan"), P("ctx", "chan")),
        check_vma=False,
    )
```

```python
import jax
import jax.numpy as jnp
import numpy as np
from jax import lax
from jax.sharding import PartitionSpec as P

block_rows = 64


def passed_along(value, axis, steps):
    count = lax.axis_size(axis)
    initial, last = (max(0, -steps), min(count, count - steps))
    return lax.ppermute(value, axis, [(source, source + steps) for source in range(initial, last)])


def prefix_scan(value, decay_one, axis, direction):
    count = lax.axis_size(axis)
    state = passed_along(value, axis, direction)
    factor, step = decay_one, 1
    while step < count:
        state = state + factor * passed_along(state, axis, step * direction)
        factor, step = factor * factor, step * 2
    return state


def on_device(gated_input, query, out_grad, out_weight, decay_rate, residue):
    tok_rows, chan_width = gated_input.shape
    block_count = tok_rows // block_rows
    lag_steps = jnp.arange(block_rows, dtype=jnp.float32)
    filter_taps = jnp.sum(
        residue[None] * jnp.exp(-decay_rate[None] * lag_steps[:, None, None]), axis=1
    )
    lag_offsets = np.arange(block_rows)[:, None] - np.arange(block_rows)[None, :]
    lag_table = np.where(lag_offsets >= 0, lag_offsets, block_rows).reshape(-1).astype(np.int32)
    padded_taps = jnp.concatenate([filter_taps, jnp.zeros((1, chan_width), jnp.float32)], axis=0)
    toeplitz = jnp.take(padded_taps, jnp.asarray(lag_table), axis=0).reshape(
        block_rows, block_rows, chan_width
    )
    to_end = jnp.exp(-decay_rate[None] * (block_rows - 1.0 - lag_steps)[:, None, None])
    from_start = jnp.exp(-decay_rate[None] * lag_steps[:, None, None])
    into_rows = residue[None] * jnp.exp(-decay_rate[None] * (lag_steps + 1.0)[:, None, None])
    back_rows = residue[None] * jnp.exp(-decay_rate[None] * (block_rows - lag_steps)[:, None, None])
    block_index = jnp.arange(block_count, dtype=jnp.float32)
    state_index = jnp.arange(block_count + 1, dtype=jnp.float32)
    gap_blocks = state_index[:, None] - 1.0 - block_index[None, :]
    fwd_coef = jnp.where(
        (gap_blocks >= 0.0)[:, :, None, None],
        jnp.exp(
            -decay_rate[None, None] * block_rows * jnp.maximum(gap_blocks, 0.0)[:, :, None, None]
        ),
        0.0,
    )
    back_coef = fwd_coef[::-1, ::-1]
    chain_decay = jnp.exp(-decay_rate * tok_rows)
    zero_state = jnp.zeros_like(chain_decay)
    input_blocks = gated_input.astype(jnp.float32).reshape(block_count, block_rows, chan_width)
    local_part = jnp.sum(toeplitz[None] * input_blocks[:, None], axis=2)
    block_ends = jnp.sum(to_end[None] * input_blocks[:, :, None], axis=1)
    block_states = jnp.sum(fwd_coef * block_ends[None], axis=1)
    local_end = block_states[block_count]

    earlier_state = prefix_scan(local_end, chain_decay, "ctx", 1)
    start_states = (
        block_states[:block_count]
        + jnp.exp(-decay_rate[None] * block_rows * block_index[:, None, None]) * earlier_state[None]
    )
    carried = jnp.sum(into_rows[None] * start_states[:, None], axis=2)
    conv_out = (local_part + carried).reshape(tok_rows, chan_width)
    grad_rows = lax.all_gather(out_grad, "chan", axis=1, tiled=True)
    grad_mixed = lax.dot_general(
        grad_rows,
        lax.all_gather(out_weight, "ctx", axis=1, tiled=True),
        (((1,), (1,)), ((), ())),
        preferred_element_type=jnp.float32,
    )
    grad_query = (grad_mixed * conv_out).astype(jnp.bfloat16)
    grad_conv = (grad_mixed * query.astype(jnp.float32)).reshape(
        block_count, block_rows, chan_width
    )
    local_back = jnp.sum(toeplitz[None] * grad_conv[:, :, None], axis=1)
    block_heads = jnp.sum(from_start[None] * grad_conv[:, :, None], axis=1)
    block_tails = jnp.sum(back_coef * block_heads[None], axis=1)
    local_out = block_tails[0]

    later_state = prefix_scan(local_out, chain_decay, "ctx", -1)
    end_states = (
        block_tails[1:]
        + jnp.exp(-decay_rate[None] * block_rows * (block_count - 1.0 - block_index)[:, None, None])
        * later_state[None]
    )
    carried_back = jnp.sum(back_rows[None] * end_states[:, None], axis=2)
    grad_input = (local_back + carried_back).reshape(tok_rows, chan_width).astype(jnp.bfloat16)
    return (grad_query, grad_input)


def solution(mesh):
    return jax.shard_map(
        on_device,
        mesh=mesh,
        in_specs=(
            P("ctx", "chan"),
            P("ctx", "chan"),
            P("ctx", "chan"),
            P("chan", "ctx"),
            P(None, "chan"),
            P(None, "chan"),
        ),
        out_specs=(P("ctx", "chan"), P("ctx", "chan")),
        check_vma=False,
    )
```

```python
import jax
import jax.numpy as jnp
import numpy as np
from jax import lax
from jax.sharding import PartitionSpec as P

block_rows = 32


def passed_along(value, axis, steps):
    count = lax.axis_size(axis)
    initial, last = (max(0, -steps), min(count, count - steps))
    return lax.ppermute(value, axis, [(source, source + steps) for source in range(initial, last)])


def prefix_scan(value, decay_one, axis, direction):
    count = lax.axis_size(axis)
    state = passed_along(value, axis, direction)
    factor, step = decay_one, 1
    while step < count:
        state = state + factor * passed_along(state, axis, step * direction)
        factor, step = factor * factor, step * 2
    return state


def on_device(gated_input, query, out_grad, out_weight, decay_rate, residue):
    tok_rows, chan_width = gated_input.shape
    block_count = tok_rows // block_rows
    lag_steps = jnp.arange(block_rows, dtype=jnp.float32)
    filter_taps = jnp.sum(
        residue[None] * jnp.exp(-decay_rate[None] * lag_steps[:, None, None]), axis=1
    )
    lag_offsets = np.arange(block_rows)[:, None] - np.arange(block_rows)[None, :]
    lag_table = np.where(lag_offsets >= 0, lag_offsets, block_rows).reshape(-1).astype(np.int32)
    padded_taps = jnp.concatenate([filter_taps, jnp.zeros((1, chan_width), jnp.float32)], axis=0)
    toeplitz = jnp.take(padded_taps, jnp.asarray(lag_table), axis=0).reshape(
        block_rows, block_rows, chan_width
    )
    to_end = jnp.exp(-decay_rate[None] * (block_rows - 1.0 - lag_steps)[:, None, None])
    from_start = jnp.exp(-decay_rate[None] * lag_steps[:, None, None])
    into_rows = residue[None] * jnp.exp(-decay_rate[None] * (lag_steps + 1.0)[:, None, None])
    back_rows = residue[None] * jnp.exp(-decay_rate[None] * (block_rows - lag_steps)[:, None, None])
    block_index = jnp.arange(block_count, dtype=jnp.float32)
    state_index = jnp.arange(block_count + 1, dtype=jnp.float32)
    gap_blocks = state_index[:, None] - 1.0 - block_index[None, :]
    fwd_coef = jnp.where(
        (gap_blocks >= 0.0)[:, :, None, None],
        jnp.exp(
            -decay_rate[None, None] * block_rows * jnp.maximum(gap_blocks, 0.0)[:, :, None, None]
        ),
        0.0,
    )
    back_coef = fwd_coef[::-1, ::-1]
    chain_decay = jnp.exp(-decay_rate * tok_rows)
    zero_state = jnp.zeros_like(chain_decay)
    input_blocks = gated_input.astype(jnp.float32).reshape(block_count, block_rows, chan_width)
    local_part = jnp.sum(toeplitz[None] * input_blocks[:, None], axis=2)
    block_ends = jnp.sum(to_end[None] * input_blocks[:, :, None], axis=1)
    block_states = jnp.sum(fwd_coef * block_ends[None], axis=1)
    local_end = block_states[block_count]

    earlier_state = prefix_scan(local_end, chain_decay, "ctx", 1)
    start_states = (
        block_states[:block_count]
        + jnp.exp(-decay_rate[None] * block_rows * block_index[:, None, None]) * earlier_state[None]
    )
    carried = jnp.sum(into_rows[None] * start_states[:, None], axis=2)
    conv_out = (local_part + carried).reshape(tok_rows, chan_width)
    grad_rows = lax.all_gather(out_grad, "chan", axis=1, tiled=True)
    grad_mixed = lax.dot_general(
        grad_rows,
        lax.all_gather(out_weight, "ctx", axis=1, tiled=True),
        (((1,), (1,)), ((), ())),
        preferred_element_type=jnp.float32,
    )
    grad_query = (grad_mixed * conv_out).astype(jnp.bfloat16)
    grad_conv = (grad_mixed * query.astype(jnp.float32)).reshape(
        block_count, block_rows, chan_width
    )
    local_back = jnp.sum(toeplitz[None] * grad_conv[:, :, None], axis=1)
    block_heads = jnp.sum(from_start[None] * grad_conv[:, :, None], axis=1)
    block_tails = jnp.sum(back_coef * block_heads[None], axis=1)
    local_out = block_tails[0]

    later_state = prefix_scan(local_out, chain_decay, "ctx", -1)
    end_states = (
        block_tails[1:]
        + jnp.exp(-decay_rate[None] * block_rows * (block_count - 1.0 - block_index)[:, None, None])
        * later_state[None]
    )
    carried_back = jnp.sum(back_rows[None] * end_states[:, None], axis=2)
    grad_input = (local_back + carried_back).reshape(tok_rows, chan_width).astype(jnp.bfloat16)
    return (grad_query, grad_input)


def solution(mesh):
    return jax.shard_map(
        on_device,
        mesh=mesh,
        in_specs=(
            P("ctx", "chan"),
            P("ctx", "chan"),
            P("ctx", "chan"),
            P("chan", "ctx"),
            P(None, "chan"),
            P(None, "chan"),
        ),
        out_specs=(P("ctx", "chan"), P("ctx", "chan")),
        check_vma=False,
    )
```

```python
import jax
import jax.numpy as jnp
import numpy as np
from jax import lax
from jax.sharding import PartitionSpec as P

block_rows = 16


def passed_along(value, axis, steps):
    count = lax.axis_size(axis)
    initial, last = (max(0, -steps), min(count, count - steps))
    return lax.ppermute(value, axis, [(source, source + steps) for source in range(initial, last)])


def prefix_scan(value, decay_one, axis, direction):
    count = lax.axis_size(axis)
    state = passed_along(value, axis, direction)
    factor, step = decay_one, 1
    while step < count:
        state = state + factor * passed_along(state, axis, step * direction)
        factor, step = factor * factor, step * 2
    return state


def on_device(gated_input, query, out_grad, out_weight, decay_rate, residue):
    tok_rows, chan_width = gated_input.shape
    block_count = tok_rows // block_rows
    lag_steps = jnp.arange(block_rows, dtype=jnp.float32)
    filter_taps = jnp.sum(
        residue[None] * jnp.exp(-decay_rate[None] * lag_steps[:, None, None]), axis=1
    )
    lag_offsets = np.arange(block_rows)[:, None] - np.arange(block_rows)[None, :]
    lag_table = np.where(lag_offsets >= 0, lag_offsets, block_rows).reshape(-1).astype(np.int32)
    padded_taps = jnp.concatenate([filter_taps, jnp.zeros((1, chan_width), jnp.float32)], axis=0)
    toeplitz = jnp.take(padded_taps, jnp.asarray(lag_table), axis=0).reshape(
        block_rows, block_rows, chan_width
    )
    to_end = jnp.exp(-decay_rate[None] * (block_rows - 1.0 - lag_steps)[:, None, None])
    from_start = jnp.exp(-decay_rate[None] * lag_steps[:, None, None])
    into_rows = residue[None] * jnp.exp(-decay_rate[None] * (lag_steps + 1.0)[:, None, None])
    back_rows = residue[None] * jnp.exp(-decay_rate[None] * (block_rows - lag_steps)[:, None, None])
    block_index = jnp.arange(block_count, dtype=jnp.float32)
    state_index = jnp.arange(block_count + 1, dtype=jnp.float32)
    gap_blocks = state_index[:, None] - 1.0 - block_index[None, :]
    fwd_coef = jnp.where(
        (gap_blocks >= 0.0)[:, :, None, None],
        jnp.exp(
            -decay_rate[None, None] * block_rows * jnp.maximum(gap_blocks, 0.0)[:, :, None, None]
        ),
        0.0,
    )
    back_coef = fwd_coef[::-1, ::-1]
    chain_decay = jnp.exp(-decay_rate * tok_rows)
    zero_state = jnp.zeros_like(chain_decay)
    input_blocks = gated_input.astype(jnp.float32).reshape(block_count, block_rows, chan_width)
    local_part = jnp.sum(toeplitz[None] * input_blocks[:, None], axis=2)
    block_ends = jnp.sum(to_end[None] * input_blocks[:, :, None], axis=1)
    block_states = jnp.sum(fwd_coef * block_ends[None], axis=1)
    local_end = block_states[block_count]

    earlier_state = prefix_scan(local_end, chain_decay, "ctx", 1)
    start_states = (
        block_states[:block_count]
        + jnp.exp(-decay_rate[None] * block_rows * block_index[:, None, None]) * earlier_state[None]
    )
    carried = jnp.sum(into_rows[None] * start_states[:, None], axis=2)
    conv_out = (local_part + carried).reshape(tok_rows, chan_width)
    grad_rows = lax.all_gather(out_grad, "chan", axis=1, tiled=True)
    grad_mixed = lax.dot_general(
        grad_rows,
        lax.all_gather(out_weight, "ctx", axis=1, tiled=True),
        (((1,), (1,)), ((), ())),
        preferred_element_type=jnp.float32,
    )
    grad_query = (grad_mixed * conv_out).astype(jnp.bfloat16)
    grad_conv = (grad_mixed * query.astype(jnp.float32)).reshape(
        block_count, block_rows, chan_width
    )
    local_back = jnp.sum(toeplitz[None] * grad_conv[:, :, None], axis=1)
    block_heads = jnp.sum(from_start[None] * grad_conv[:, :, None], axis=1)
    block_tails = jnp.sum(back_coef * block_heads[None], axis=1)
    local_out = block_tails[0]

    later_state = prefix_scan(local_out, chain_decay, "ctx", -1)
    end_states = (
        block_tails[1:]
        + jnp.exp(-decay_rate[None] * block_rows * (block_count - 1.0 - block_index)[:, None, None])
        * later_state[None]
    )
    carried_back = jnp.sum(back_rows[None] * end_states[:, None], axis=2)
    grad_input = (local_back + carried_back).reshape(tok_rows, chan_width).astype(jnp.bfloat16)
    return (grad_query, grad_input)


def solution(mesh):
    return jax.shard_map(
        on_device,
        mesh=mesh,
        in_specs=(
            P("ctx", "chan"),
            P("ctx", "chan"),
            P("ctx", "chan"),
            P("chan", "ctx"),
            P(None, "chan"),
            P(None, "chan"),
        ),
        out_specs=(P("ctx", "chan"), P("ctx", "chan")),
        check_vma=False,
    )
```
